32 devices in a mesh: seq: 8 (over z, x), qblk: 4 (over y, core).
Axes of the slice: x: 2, y: 2, z: 4, core: 2. Of those that a mesh axis runs over, the one named last changes fastest.
Arguments:
- queries: bfloat16 [4096, 8192], P(('seq', 'qblk')), may hold values from -33 to 33
- key_states: bfloat16 [4096, 1024], P(('seq', 'qblk')), may hold values from -6 to 6
- value_states: bfloat16 [4096, 1024], P(('seq', 'qblk')), may hold values from -6 to 6
- block_list: int32 [64, 32, 16], replicated, may hold values from 0 to 31, as said below
- block_count: int32 [64, 32], replicated, may hold values from 1 to 16, as said below
Outputs:
- attended: bfloat16 [4096, 8192], P(('seq', 'qblk'))
The draws below stay inside these ranges and needn't reach their ends.
Inputs may be any that keep to these rules, and one draw needn't show every extreme that they name: `block_list`: for each head and query block, the first block_count entries are distinct key blocks no later than the query block, among them the query block itself; the remaining entries are 0. block_count[h, i] <= i + 1.
All inputs are finite; a program needn't handle non-finite values.
Results may differ from the reference program's by a relative error of at most 0.0044.
Values may be sent and summed in bfloat16 or wider, within the bound.
A program may use at most 64 MiB of HBM per device.

```python
import jax
import jax.numpy as jnp
from jax import lax

H = 64
KVH = 8
HEAD_SIZE = 128
BLK = 128
MAXB = 16
SEQ = 4096
NQB = 32


def list_parts(key):
    folded = jax.random.fold_in(key, 101)
    k_vert, k_rand, k_low, k_len = jax.random.split(folded, 4)
    query_ids = jnp.arange(NQB, dtype=jnp.int32)[None, :, None]
    key_ids = jnp.arange(NQB, dtype=jnp.int32)[None, None, :]
    vertical = jax.random.randint(k_vert, (H, 2, 1, 1), 0, NQB)
    priority = 1 + 8 * (key_ids == query_ids).astype(jnp.int32) + 2 * (key_ids == 0).astype(jnp.int32) + (key_ids == query_ids - 1).astype(jnp.int32) + (key_ids == vertical[:, 0]).astype(jnp.int32) + (key_ids == vertical[:, 1]).astype(jnp.int32)
    jitter = jax.random.randint(k_rand, (H, NQB, NQB), 0, 4096)
    ranking = jnp.where(key_ids <= query_ids, priority * 16777216 + jitter * 2048 + key_ids, -1 - key_ids)
    chosen = lax.top_k(ranking, MAXB)[1].astype(jnp.int32)
    floor_len = jax.random.randint(k_low, (H, 1), max(MAXB // 4, 2), MAXB + 1)
    length = jax.random.randint(k_len, (H, NQB), floor_len, MAXB + 1)
    query_col = jnp.arange(NQB, dtype=jnp.int32)[None, :]
    length = jnp.where(query_col == NQB - 1, MAXB, length)
    counts_all = jnp.minimum(length, query_col + 1).astype(jnp.int32)
    slot_ids = jnp.arange(MAXB, dtype=jnp.int32)[None, None, :]
    chosen = jnp.where(slot_ids < counts_all[:, :, None], chosen, 0).astype(jnp.int32)
    return (chosen, counts_all)


def draw_block_list(key, part):
    return list_parts(key)[0]


def draw_block_count(key, part):
    return list_parts(key)[1]


def vector_parts(key):
    folded = jax.random.fold_in(key, 202)
    k_key, k_query = jax.random.split(folded, 2)
    keys_final = jnp.clip(jax.random.normal(k_key, (SEQ, KVH * HEAD_SIZE), jnp.float32), -6.0, 6.0)
    queries_final = jnp.clip(jax.random.normal(k_query, (SEQ, H * HEAD_SIZE), jnp.float32), -6.0, 6.0)
    return (queries_final, keys_final)


def draw_queries(key, part):
    return vector_parts(key)[0].astype(jnp.bfloat16)


def draw_key_states(key, part):
    return vector_parts(key)[1].astype(jnp.bfloat16)


def block_scale(stream_key, dims, pieces, low, high):
    loudness, own = 1.0, jax.random.fold_in(stream_key, 6)
    for position, blocks in pieces:
        heights = jnp.exp(jax.random.uniform(jax.random.fold_in(own, position), (blocks,), jnp.float32, low / len(pieces), high / len(pieces)))
        loudness = loudness * jnp.repeat(heights, dims[position] // blocks).reshape([-1 if axis == position else 1 for axis in range(len(dims))])
    return loudness


def bell_draw(stream_key, extent, spread, most, cuts=(), kind=jnp.bfloat16):
    entries = spread * jax.random.normal(stream_key, extent, jnp.float32)
    if cuts:
        entries = entries * block_scale(stream_key, extent, cuts, -0.22, 0.18)
    return jnp.clip(entries, -most, most).astype(kind)


def setup_inputs(seed: int = 0) -> dict:
    streams_of = jax.random.split(jax.random.key(seed), 6)
    return {
        "queries": draw_queries(jax.random.fold_in(streams_of[5], 71), 0),
        "key_states": draw_key_states(jax.random.fold_in(streams_of[5], 71), 0),
        "value_states": bell_draw(streams_of[2], (SEQ, KVH * HEAD_SIZE), 1.0, 6.0, ((0, 32),)),
        "block_list": draw_block_list(jax.random.fold_in(streams_of[5], 71), 0),
        "block_count": draw_block_count(jax.random.fold_in(streams_of[5], 71), 0),
    }


def reference(queries, key_states, value_states, block_list, block_count):
    block_total = SEQ // BLK
    group_size = H // KVH
    score_scale = HEAD_SIZE ** -0.5
    query_grid = queries.reshape(block_total, BLK, H, HEAD_SIZE)
    kv_grid = jnp.concatenate([key_states.reshape(block_total, BLK, KVH, HEAD_SIZE), value_states.reshape(block_total, BLK, KVH, HEAD_SIZE)], axis=3)
    query_pos = jnp.arange(block_total, dtype=jnp.int32)[:, None, None, None] * BLK + jnp.arange(BLK, dtype=jnp.int32)[None, :, None, None]
    slot_ids = jnp.arange(MAXB, dtype=jnp.int32)[None, None, :, None]
    inner_pos = jnp.arange(BLK, dtype=jnp.int32)[None, None, None, :]

    def per_head(head_id):
        query_head = lax.dynamic_index_in_dim(query_grid, head_id, axis=2, keepdims=False).astype(jnp.float32)
        kv_head = lax.dynamic_index_in_dim(kv_grid, head_id // group_size, axis=2, keepdims=False)
        indices = lax.dynamic_index_in_dim(block_list, head_id, axis=0, keepdims=False).astype(jnp.int32)
        counts_now = lax.dynamic_index_in_dim(block_count, head_id, axis=0, keepdims=False).astype(jnp.int32)
        key_value_tiles = kv_head[indices]
        attention_scores = jnp.einsum("psi,pcai->psca", query_head, key_value_tiles[..., :HEAD_SIZE].astype(jnp.float32)) * score_scale
        key_pos = indices[:, None, :, None] * BLK + inner_pos
        usable = (slot_ids < counts_now[:, None, None, None]) & (key_pos <= query_pos)
        attention_scores = jnp.where(usable, attention_scores, -jnp.inf)
        highest = jnp.max(attention_scores, axis=(2, 3), keepdims=True)
        weights = jnp.exp(attention_scores - highest)
        weight_sum = jnp.sum(weights, axis=(2, 3))
        rounded_length = lax.optimization_barrier(weights.astype(jnp.bfloat16)).astype(jnp.float32)
        combined_output = jnp.einsum("hoac,hact->hot", rounded_length, key_value_tiles[..., HEAD_SIZE:].astype(jnp.float32))
        return (combined_output / weight_sum[:, :, None]).astype(jnp.bfloat16)

    per_block = lax.map(per_head, jnp.arange(H, dtype=jnp.int32))
    return per_block.transpose(1, 2, 0, 3).reshape(SEQ, H * HEAD_SIZE)
```

```python
import functools

import jax
import jax.numpy as jnp
from jax import lax
from jax.experimental import pallas as pl
from jax.experimental.pallas import tpu as pltpu
from jax.sharding import Mesh, PartitionSpec as P

H = 64
KVH = 8
D = 128
BLK = 128
MAXB = 16
GROUP = H // KVH
HALF = KVH // 2
LOG2E = 1.4426950408889634
C = D ** (-0.5) * LOG2E
NEVER = -4 * BLK


def attend_unit(q, k_at, v_at, thr_at, diff, s_ref):
    top = None
    for j in range(MAXB // 2):
        k = jnp.concatenate([k_at(2 * j), k_at(2 * j + 1)], axis=0)
        s = lax.dot_general(q, k, (((1,), (1,)), ((), ())), preferred_element_type=jnp.float32)
        for i in range(2):
            part = s[:, i * BLK : (i + 1) * BLK]
            part = jnp.where(diff <= thr_at(2 * j + i), part, -jnp.inf)
            s_ref[:, (2 * j + i) * BLK : (2 * j + i + 1) * BLK] = part
            top = part if top is None else jnp.maximum(top, part)
    highest = jnp.max(top, axis=1, keepdims=True) * C
    total = None
    acc = None
    for j in range(MAXB // 2):
        v = jnp.concatenate([v_at(2 * j), v_at(2 * j + 1)], axis=0)
        p = jnp.exp2(s_ref[:, 2 * j * BLK : (2 * j + 2) * BLK] * C - highest)
        both = p[:, :BLK] + p[:, BLK:]
        total = both if total is None else total + both
        o = jnp.dot(p.astype(jnp.bfloat16), v, preferred_element_type=jnp.float32)
        acc = o if acc is None else acc + o
    return (acc / jnp.sum(total, axis=1, keepdims=True)).astype(jnp.bfloat16)


def attend_kernel(idx_ref, thr_ref, qa_ref, qb_ref, kv_ref, oa_ref, ob_ref, s_ref):
    h = pl.program_id(0)
    diff = lax.broadcasted_iota(jnp.int32, (BLK, BLK), 1) - lax.broadcasted_iota(
        jnp.int32, (BLK, BLK), 0
    )
    for n, (q_ref, o_ref) in enumerate(((qa_ref, oa_ref), (qb_ref, ob_ref))):
        base = (h * 2 + n) * MAXB
        o_ref[...] = attend_unit(
            q_ref[...],
            lambda m: kv_ref[idx_ref[base + m], 0],
            lambda m: kv_ref[idx_ref[base + m], 1],
            lambda m: thr_ref[base + m],
            diff,
            s_ref.at[n],
        )


def attend(idx, thr, qa, qb, kv):
    col = pl.BlockSpec((BLK, D), lambda h, *_: (0, h))
    whole = pl.BlockSpec(kv.shape, lambda h, *_: (0, 0, 0, 0))
    out = jax.ShapeDtypeStruct(qa.shape, jnp.bfloat16)
    units = 2 * GROUP * MAXB * BLK * BLK
    return pl.pallas_call(
        attend_kernel,
        grid_spec=pltpu.PrefetchScalarGridSpec(
            num_scalar_prefetch=2,
            grid=(GROUP,),
            in_specs=[col, col, whole],
            out_specs=[col, col],
            scratch_shapes=[pltpu.VMEM((2, BLK, MAXB * BLK), jnp.float32)],
        ),
        out_shape=[out, out],
        cost_estimate=pl.CostEstimate(
            flops=4 * units * D, bytes_accessed=kv.size * 2, transcendentals=units
        ),
        name="attend",
    )(idx, thr, qa, qb, kv)


def shards(q, k, v, block_list, block_count):
    c = lax.axis_index("core")
    chip = lax.axis_index("seq") * lax.axis_size("y") + lax.axis_index("y")
    swap = [(0, 1), (1, 0)]

    def halves(x):
        w = x.shape[1] // 2
        return (
            lax.dynamic_slice_in_dim(x, c * w, w, 1),
            lax.dynamic_slice_in_dim(x, (1 - c) * w, w, 1),
        )

    kv = jnp.stack([k.reshape(BLK, KVH, D), v.reshape(BLK, KVH, D)], axis=0)
    kv = kv.transpose(2, 0, 1, 3).reshape(2, HALF, 2, BLK, D)
    kv_mine = lax.dynamic_index_in_dim(kv, c, 0, keepdims=False)
    kv_sent = lax.dynamic_index_in_dim(kv, 1 - c, 0, keepdims=False)
    kv_got = lax.ppermute(kv_sent, "core", swap)
    qa, q_sent = halves(q)
    qb = lax.ppermute(q_sent, "core", swap)
    pair = jnp.stack([kv_mine, kv_got], axis=1)

    lists = lax.dynamic_slice_in_dim(block_list, c * (H // 2), H // 2, 0)
    counts = lax.dynamic_slice_in_dim(block_count, c * (H // 2), H // 2, 0)
    blocks = jnp.stack([2 * chip + c, 2 * chip + 1 - c])
    lists = jnp.stack([lists[:, blocks[0]], lists[:, blocks[1]]], axis=1)
    counts = jnp.stack([counts[:, blocks[0]], counts[:, blocks[1]]], axis=1)
    slots = jnp.arange(MAXB, dtype=jnp.int32)
    thr = jnp.where(
        slots < counts[:, :, None], (blocks[None, :, None] - lists) * BLK, NEVER
    ).reshape(HALF, -1)
    idx = ((lists // 2) * 2 + (lists % 2 + c) % 2).reshape(HALF, -1)

    oa, ob = [], []
    for g in range(HALF):
        gathered = lax.all_gather(pair[g], ("seq", "y"), axis=0, tiled=True)
        w = GROUP * D
        a, b = attend(
            idx[g], thr[g], qa[:, g * w : (g + 1) * w], qb[:, g * w : (g + 1) * w], gathered
        )
        oa.append(a)
        ob.append(b)
    mine = jnp.concatenate(oa, axis=1)
    got = lax.ppermute(jnp.concatenate(ob, axis=1), "core", swap)
    low = jnp.where(c == 0, mine, got)
    high = jnp.where(c == 0, got, mine)
    return jnp.concatenate([low, high], axis=1)


def solution(mesh):
    n_seq, n_qblk = mesh.devices.shape
    fine = Mesh(mesh.devices.reshape(n_seq, n_qblk // 2, 2), ("seq", "y", "core"))
    rows = P(("seq", "y", "core"), None)
    return jax.shard_map(
        shards,
        mesh=fine,
        in_specs=(rows, rows, rows, P(), P()),
        out_specs=rows,
        check_vma=False,
    )
```

```python
import functools

import jax
import jax.numpy as jnp
from jax import lax
from jax.experimental import pallas as pl
from jax.experimental.pallas import tpu as pltpu
from jax.sharding import Mesh, PartitionSpec as P

H = 64
KVH = 8
D = 128
BLK = 128
MAXB = 16
GROUP = H // KVH
HALF = KVH // 2
LOG2E = 1.4426950408889634
C = D ** (-0.5) * LOG2E
NEVER = -4 * BLK


def attend_unit(q, k_at, v_at, thr_at, diff, s_ref):
    top = None
    for j in range(MAXB // 2):
        k = jnp.concatenate([k_at(2 * j), k_at(2 * j + 1)], axis=0)
        s = lax.dot_general(q, k, (((1,), (1,)), ((), ())), preferred_element_type=jnp.float32)
        for i in range(2):
            part = s[:, i * BLK : (i + 1) * BLK]
            part = jnp.where(diff <= thr_at(2 * j + i), part, -jnp.inf)
            s_ref[:, (2 * j + i) * BLK : (2 * j + i + 1) * BLK] = part
            top = part if top is None else jnp.maximum(top, part)
    highest = jnp.max(top, axis=1, keepdims=True) * C
    total = None
    acc = None
    for j in range(MAXB // 2):
        v = jnp.concatenate([v_at(2 * j), v_at(2 * j + 1)], axis=0)
        p = jnp.exp2(s_ref[:, 2 * j * BLK : (2 * j + 2) * BLK] * C - highest)
        both = p[:, :BLK] + p[:, BLK:]
        total = both if total is None else total + both
        o = jnp.dot(p.astype(jnp.bfloat16), v, preferred_element_type=jnp.float32)
        acc = o if acc is None else acc + o
    return (acc / jnp.sum(total, axis=1, keepdims=True)).astype(jnp.bfloat16)


ORDERS = ((0, 1, 2), (0, 2, 1), (0, 1, 2), (0, 2, 1), (1, 2, 0), (2, 1, 0), (0, 1, 2), (0, 2, 1))
SKEW = 2


def fused_kernel(sizes, idx_ref, thr_ref, qa_ref, qb_ref, pair_ref, oa_ref, ob_ref, *scratch):
    bufs = scratch[: 2 * HALF]
    s_ref, own_sem, send_sem, recv_sem = scratch[2 * HALF :]
    nb, ny = sizes[1], sizes[2]
    seq = lax.axis_index("seq")
    me = (seq // nb, seq % nb, lax.axis_index("y"))

    def target(dim, to):
        if dim == 2:
            return {"y": to}
        return {"seq": to * nb + me[1] if dim == 0 else me[0] * nb + to}

    barrier = pltpu.get_barrier_semaphore()
    expected = 0
    for dim in range(3):
        for way in (1, -1):
            to = me[dim] + way
            there = (to >= 0) & (to < sizes[dim])
            expected = expected + there.astype(jnp.int32)

            @pl.when(there)
            def _():
                pl.semaphore_signal(
                    barrier, inc=1, device_id=target(dim, to), device_id_type=pl.DeviceIdType.MESH
                )

    own = []
    for u in range(2 * HALF):
        copy = pltpu.make_async_copy(
            pair_ref.at[u // 2, u % 2], bufs[u].at[me[0], me[1], me[2]], own_sem.at[u]
        )
        copy.start()
        own.append(copy)
    pl.semaphore_wait(barrier, expected)

    offsets = {}
    slots = 0
    for u in range(2 * HALF):
        for dim in range(3):
            offsets[u, dim] = slots
            slots += 2 * (sizes[dim] - 1)

    def copy_of(u, stage, way, k):
        dim = ORDERS[u][stage]
        done = ORDERS[u][:stage]
        piece = me[dim] - way * k
        region = tuple(
            slice(None) if d in done else (piece if d == dim else me[d]) for d in range(3)
        )
        slot = offsets[u, dim] + 2 * k + (0 if way == 1 else 1)
        sent = (me[dim] + way >= 0) & (me[dim] + way < sizes[dim])
        held = (piece >= 0) & (piece < sizes[dim])
        came = me[dim] - way * (k + 1)
        return (
            pltpu.make_async_remote_copy(
                src_ref=bufs[u].at[region],
                dst_ref=bufs[u].at[region],
                send_sem=send_sem.at[slot],
                recv_sem=recv_sem.at[slot],
                device_id=target(dim, me[dim] + way),
                device_id_type=pl.DeviceIdType.MESH,
            ),
            sent & held,
            (came >= 0) & (came < sizes[dim]),
        )

    def send(u, stage, k):
        for way in (1, -1):
            copy, sends, _ = copy_of(u, stage, way, k)
            pl.when(sends)(copy.start)

    def receive(u, stage, k):
        for way in (1, -1):
            copy, _, comes = copy_of(u, stage, way, k)
            pl.when(comes)(copy.wait_recv)

    plans = []
    for u in range(2 * HALF):
        plan = [(None, None, 0, 0)]
        for stage in range(3):
            n = sizes[ORDERS[u][stage]]
            for k in range(n - 1):
                after = (stage, k + 1) if k + 1 < n - 1 else (stage + 1, 0)
                plan.append((stage, k, *after))
        plans.append(plan)

    def advance(u, i):
        stage, k, next_stage, next_k = plans[u][i]
        if stage is None:
            own[u].wait()
        else:
            receive(u, stage, k)
        if next_stage < 3:
            send(u, next_stage, next_k)

    diff = lax.broadcasted_iota(jnp.int32, (BLK, BLK), 1) - lax.broadcasted_iota(
        jnp.int32, (BLK, BLK), 0
    )

    def attend(g, low, high):
        def at(buf, i):
            return buf[i // (2 * nb * ny), (i // (2 * ny)) % nb, (i // 2) % ny, i % 2]

        def step(h, _):
            cols = pl.ds(pl.multiple_of(h * D, D), D)
            for n, (q_ref, o_ref) in enumerate(((qa_ref, oa_ref), (qb_ref, ob_ref))):
                base = (h * 2 + n) * MAXB
                at_slot = [idx_ref[base + m].astype(jnp.uint32) for m in range(MAXB)]
                o_ref[:, cols] = attend_unit(
                    q_ref[:, cols],
                    lambda m: at(bufs[2 * g], at_slot[m]),
                    lambda m: at(bufs[2 * g + 1], at_slot[m]),
                    lambda m: thr_ref[base + m],
                    diff,
                    s_ref.at[n],
                )
            return 0

        lax.fori_loop(g * GROUP + low, g * GROUP + high, step, 0)

    length = len(plans[0])
    last = (HALF - 1) * SKEW + length
    todo = []
    for wave in range(last):
        if todo:
            attend(*todo.pop(0))
        for g in range(HALF):
            i = wave - g * SKEW
            if 0 <= i < length:
                advance(2 * g, i)
                advance(2 * g + 1, i)
                if i == length - 1:
                    step = GROUP // SKEW
                    todo += [(g, j * step, (j + 1) * step) for j in range(SKEW)]
    g = HALF - 1
    for item in todo[:-SKEW]:
        attend(*item)
    attend(g, 0, GROUP)

    for u in range(2 * HALF):
        for stage in range(3):
            for k in range(sizes[ORDERS[u][stage]] - 1):
                for way in (1, -1):
                    copy, sends, _ = copy_of(u, stage, way, k)
                    pl.when(sends)(copy.wait_send)


def fused(sizes, idx, thr, qa, qb, pair):
    vmem = pl.BlockSpec(memory_space=pltpu.VMEM)
    smem = pl.BlockSpec(memory_space=pltpu.SMEM)
    out = jax.ShapeDtypeStruct(qa.shape, jnp.bfloat16)
    buf = pltpu.VMEM((*sizes, 2, BLK, D), jnp.bfloat16)
    slots = 2 * HALF * 2 * (sum(sizes) - 3)
    return pl.pallas_call(
        functools.partial(fused_kernel, sizes),
        in_specs=[smem, smem, vmem, vmem, vmem],
        out_specs=[vmem, vmem],
        scratch_shapes=[buf] * (2 * HALF)
        + [
            pltpu.VMEM((2, BLK, MAXB * BLK), jnp.float32),
            pltpu.SemaphoreType.DMA((2 * HALF,)),
            pltpu.SemaphoreType.DMA((slots,)),
            pltpu.SemaphoreType.DMA((slots,)),
        ],
        out_shape=[out, out],
        compiler_params=pltpu.CompilerParams(collective_id=0, has_side_effects=True),
        name="gather_attend",
    )(idx, thr, qa, qb, pair)


def shards(q, k, v, block_list, block_count):
    c = lax.axis_index("core")
    chip = lax.axis_index("seq") * lax.axis_size("y") + lax.axis_index("y")
    swap = [(0, 1), (1, 0)]

    def halves(x):
        w = x.shape[1] // 2
        return (
            lax.dynamic_slice_in_dim(x, c * w, w, 1),
            lax.dynamic_slice_in_dim(x, (1 - c) * w, w, 1),
        )

    kv = jnp.stack([k.reshape(BLK, KVH, D), v.reshape(BLK, KVH, D)], axis=0)
    kv = kv.transpose(2, 0, 1, 3).reshape(2, HALF, 2, BLK, D)
    kv_mine = lax.dynamic_index_in_dim(kv, c, 0, keepdims=False)
    kv_sent = lax.dynamic_index_in_dim(kv, 1 - c, 0, keepdims=False)
    kv_got = lax.ppermute(kv_sent, "core", swap)
    qa, q_sent = halves(q)
    qb = lax.ppermute(q_sent, "core", swap)
    pair = jnp.stack([kv_mine, kv_got], axis=2)

    lists = lax.dynamic_slice_in_dim(block_list, c * (H // 2), H // 2, 0)
    counts = lax.dynamic_slice_in_dim(block_count, c * (H // 2), H // 2, 0)
    blocks = jnp.stack([2 * chip + c, 2 * chip + 1 - c])
    lists = jnp.stack([lists[:, blocks[0]], lists[:, blocks[1]]], axis=1)
    counts = jnp.stack([counts[:, blocks[0]], counts[:, blocks[1]]], axis=1)
    slots = jnp.arange(MAXB, dtype=jnp.int32)
    thr = jnp.where(
        slots < counts[:, :, None], (blocks[None, :, None] - lists) * BLK, NEVER
    ).reshape(-1)
    idx = ((lists // 2) * 2 + (lists % 2 + c) % 2).reshape(-1)

    nb = lax.axis_size("seq") // 4
    mine, sent = fused((4, nb, lax.axis_size("y")), idx, thr, qa, qb, pair)
    got = lax.ppermute(sent, "core", swap)
    low = jnp.where(c == 0, mine, got)
    high = jnp.where(c == 0, got, mine)
    return jnp.concatenate([low, high], axis=1)


def solution(mesh):
    n_seq, n_qblk = mesh.devices.shape
    fine = Mesh(mesh.devices.reshape(n_seq, n_qblk // 2, 2), ("seq", "y", "core"))
    rows = P(("seq", "y", "core"), None)
    return jax.shard_map(
        shards,
        mesh=fine,
        in_specs=(rows, rows, rows, P(), P()),
        out_specs=rows,
        check_vma=False,
    )
```
